32 devices in a mesh: ctx: 8 (over z, y), head: 4 (over x, core).
Axes of the slice: x: 2, y: 2, z: 4, core: 2. Of those that a mesh axis runs over, the one named last changes fastest.
Arguments:
- query_rows: bfloat16 [1024, 4096], P('ctx', 'head'), may hold values from -0.3125 to 0.3125
- key_rows: bfloat16 [1024, 4096], P('ctx', 'head'), may hold values from -0.3125 to 0.3125
- value_rows: bfloat16 [1024, 4096], P('ctx', 'head'), may hold values from -0.3125 to 0.3125
- out_grad: bfloat16 [1024, 4096], P('ctx', 'head'), may hold values from -6 to 6
Outputs:
- grad_query: float32 [1024, 4096], P('ctx', 'head')
- grad_key: float32 [1024, 4096], P('ctx', 'head')
- grad_value: float32 [1024, 4096], P('ctx', 'head')
The draws below stay inside these ranges and needn't reach their ends.
All inputs are finite; a program needn't handle non-finite values.
Results may differ from the reference program's by a relative error of at most 0.0029.
Values sent between devices are 32-bit elements; how exact they have to be, the bound alone decides.
A program may use at most 128 MiB of HBM per device.

```python
import jax
import jax.numpy as jnp
from jax import lax

HEADS = 32
DH = 128
TOK_DEV = 128
TOKENS = 1024
N_CTX = 8


def shard_levels(own_key, dims, cuts, least, top_value):
    loudness, own = 1.0, jax.random.fold_in(own_key, 6)
    for axis_at, blocks in cuts:
        steps = jnp.exp(jax.random.uniform(jax.random.fold_in(own, axis_at), (blocks,), jnp.float32, least / len(cuts), top_value / len(cuts)))
        loudness = loudness * jnp.repeat(steps, dims[axis_at] // blocks).reshape([-1 if axis == axis_at else 1 for axis in range(len(dims))])
    return loudness


def noise(own_key, shape, scale, most, cuts=(), held_as=jnp.bfloat16):
    values = jax.random.normal(own_key, shape, jnp.float32) * scale
    if len(cuts) > 0:
        values = shard_levels(own_key, shape, cuts, -0.22, 0.18) * values
    return jnp.clip(values, min=-most, max=most).astype(held_as)


def setup_inputs(seed: int = 0) -> dict:
    splits = jax.random.split(jax.random.key(seed), 5)
    return {
        "query_rows": noise(splits[0], (TOKENS, HEADS * DH), ((DH * TOKENS) ** -0.25), 0.3125, ((0, 8), (1, 4))),
        "key_rows": noise(splits[1], (TOKENS, HEADS * DH), ((DH * TOKENS) ** -0.25), 0.3125, ((0, 8), (1, 4))),
        "value_rows": noise(splits[2], (TOKENS, HEADS * DH), ((DH * TOKENS) ** -0.25), 0.3125, ((0, 8), (1, 4))),
        "out_grad": noise(splits[3], (TOKENS, HEADS * DH), 1.0, 6.0, ((0, 8), (1, 4))),
    }


def blend_function(form, left, right):
    return jnp.einsum(form, left, right, precision=lax.Precision.HIGHEST)


def to_bf16(array):
    rounded = lax.optimization_barrier(array.astype(jnp.bfloat16))
    return rounded.astype(jnp.float32)


def reference(query_rows, key_rows, value_rows, out_grad):
    def split(array):
        return array.astype(jnp.float32).reshape(N_CTX, TOK_DEV, HEADS, DH)

    query_b, key_b, value_b, grad_b = split(query_rows), split(key_rows), split(value_rows), split(out_grad)
    block_state = blend_function("blhk,blhv->bhkv", key_b, value_b)
    block_grad = blend_function("blhk,blhv->bhkv", query_b, grad_b)
    zero_state = jnp.zeros_like(block_state[:1])
    prefix = jnp.concatenate([zero_state, jnp.cumsum(block_state, axis=0)[:-1]], axis=0)
    suffix_incl = jnp.flip(jnp.cumsum(jnp.flip(block_grad, 0), axis=0), 0)
    suffix = jnp.concatenate([suffix_incl[1:], zero_state], axis=0)
    prefix = to_bf16(prefix)
    suffix = to_bf16(suffix)
    later = jnp.arange(TOK_DEV)[:, None] >= jnp.arange(TOK_DEV)[None, :]

    def one_block(items):
        query_piece, key_piece, value_piece, gradient_piece, prefix_piece, suffix_piece = items
        score_matrix = blend_function("thk,shk->hts", query_piece, key_piece)
        score_matrix = to_bf16(jnp.where(later[None], score_matrix, 0.0))
        score_gradient = blend_function("thv,shv->hts", gradient_piece, value_piece)
        score_gradient = to_bf16(jnp.where(later[None], score_gradient, 0.0))
        query_gradient = blend_function("duq,qdg->udg", score_gradient, key_piece) + blend_function("yfe,foe->yfo", gradient_piece, prefix_piece)
        key_gradient = blend_function("wlf,lwa->fwa", score_gradient, query_piece) + blend_function("fdw,duw->fdu", value_piece, suffix_piece)
        value_gradient = blend_function("ulq,lug->qug", score_matrix, gradient_piece) + blend_function("zga,gau->zgu", key_piece, suffix_piece)
        return query_gradient, key_gradient, value_gradient

    query_gradient, key_gradient, value_gradient = lax.map(one_block, (query_b, key_b, value_b, grad_b, prefix, suffix))
    return (query_gradient.reshape(TOKENS, HEADS * DH), key_gradient.reshape(TOKENS, HEADS * DH), value_gradient.reshape(TOKENS, HEADS * DH))
```

```python
import functools

import jax
import jax.numpy as jnp
from jax import lax
from jax.experimental import pallas as pl
from jax.experimental.pallas import tpu as pltpu
from jax.sharding import PartitionSpec as P

DH = 128
MESH = pl.DeviceIdType.MESH
F32 = jnp.float32
BF16 = jnp.bfloat16


def dot(left, right, over_left, over_right):
    return lax.dot_general(
        left, right, (((over_left,), (over_right,)), ((), ())), preferred_element_type=F32
    )


def kernel(
    n, heads,
    q_hbm, k_hbm, v_hbm, g_hbm, dq_hbm, dk_hbm, dv_hbm,
    rows, own, partner, carry_in, carry_out, grads,
    load_sem, store_sem, swap_send, swap_recv, chain_send, chain_recv,
):
    tok = rows.shape[1]
    me = lax.axis_index("ctx")
    side = lax.rem(me, 2)
    row = me // 2
    last = n // 2 - 1
    other = me + 1 - 2 * side

    loads = [
        pltpu.make_async_copy(src, rows.at[i], load_sem.at[i])
        for i, src in enumerate((k_hbm, v_hbm, q_hbm, g_hbm))
    ]
    for load in loads:
        load.start()

    barrier = pltpu.get_barrier_semaphore()

    def greet(device):
        pl.semaphore_signal(barrier, inc=1, device_id={"ctx": device}, device_id_type=MESH)

    greet(other)

    @pl.when(row > 0)
    def _():
        greet(me - 2)

    @pl.when(row < last)
    def _():
        greet(me + 2)

    peers = 1 + jnp.where(row > 0, 1, 0) + jnp.where(row < last, 1, 0)
    pl.semaphore_wait(barrier, peers)

    for load in loads:
        load.wait()

    def swap(kind, h):
        return pltpu.make_async_remote_copy(
            src_ref=own.at[kind, h],
            dst_ref=partner.at[kind, h],
            send_sem=swap_send.at[kind, h],
            recv_sem=swap_recv.at[kind, h],
            device_id={"ctx": other},
            device_id_type=MESH,
        )

    def chain(kind, h):
        return pltpu.make_async_remote_copy(
            src_ref=carry_out.at[kind, h],
            dst_ref=carry_in.at[kind, h],
            send_sem=chain_send.at[kind, h],
            recv_sem=chain_recv.at[kind, h],
            device_id={"ctx": me + 2 - 4 * kind},
            device_id_type=MESH,
        )

    def columns(h):
        return pl.ds(pl.multiple_of(h * DH, DH), DH)

    early = jnp.where(2 * row <= last, 0, 1)

    def edge(kind):
        return jnp.where(kind == 0, last, 0)

    def begin(kind):
        return jnp.where(kind == 0, 0, last)

    def start_swaps(kind):
        needed = (row != edge(kind)) | (side == kind)

        def one(h, _):
            own[kind, h] = dot(rows[2 * kind, :, columns(h)], rows[2 * kind + 1, :, columns(h)], 0, 0)

            @pl.when(needed)
            def _():
                swap(kind, h).start()

            return 0

        lax.fori_loop(0, heads, one, 0)

    def store(i, h):
        out = (dq_hbm, dk_hbm, dv_hbm)[i]
        return pltpu.make_async_copy(
            grads.at[i, :, columns(h)], out.at[:, columns(h)], store_sem.at[i, h]
        )

    def carry(kind, h):
        takes = (row != edge(kind)) | (side == 1 - kind)

        @pl.when(takes)
        def _():
            swap(kind, h).wait_recv()

        @pl.when(row != begin(kind))
        def _():
            chain(kind, h).wait_recv()

        before = jnp.where(row != begin(kind), carry_in[kind, h], 0.0)

        @pl.when(row != edge(kind))
        def _():
            carry_out[kind, h] = before + own[kind, h] + partner[kind, h]
            chain(kind, h).start()

        total = before + jnp.where(side == 1 - kind, partner[kind, h], 0.0)
        total = total.astype(BF16)

        @pl.when(kind == 0)
        def _():
            grads[0, :, columns(h)] += dot(rows[3, :, columns(h)], total, 1, 1)
            store(0, h).start()

        @pl.when(kind == 1)
        def _():
            grads[1, :, columns(h)] += dot(rows[1, :, columns(h)], total, 1, 1)
            store(1, h).start()
            grads[2, :, columns(h)] += dot(rows[0, :, columns(h)], total, 1, 0)
            store(2, h).start()

    start_swaps(early)
    start_swaps(1 - early)

    down = lax.broadcasted_iota(jnp.int32, (tok, tok), 0)
    across = lax.broadcasted_iota(jnp.int32, (tok, tok), 1)

    def first(h, _):
        k, v, q, g = (rows[i, :, columns(h)] for i in range(4))
        dprob = jnp.where(down >= across, dot(g, v, 1, 1), 0.0).astype(BF16)
        dprob_t = jnp.where(down <= across, dot(v, g, 1, 1), 0.0).astype(BF16)
        scores_t = jnp.where(down <= across, dot(k, q, 1, 1), 0.0).astype(BF16)
        grads[0, :, columns(h)] = dot(dprob, k, 1, 0)
        grads[1, :, columns(h)] = dot(dprob_t, q, 1, 0)
        grads[2, :, columns(h)] = dot(scores_t, g, 1, 0)
        carry(early, h)
        return 0

    lax.fori_loop(0, heads, first, 0)

    def second(h, _):
        carry(1 - early, h)
        return 0

    lax.fori_loop(0, heads, second, 0)

    def drain(h, _):
        for kind in range(2):
            @pl.when((row != edge(kind)) | (side == kind))
            def _():
                swap(kind, h).wait_send()

            @pl.when(row != edge(kind))
            def _():
                chain(kind, h).wait_send()

        for i in range(3):
            store(i, h).wait()
        return 0

    lax.fori_loop(0, heads, drain, 0)


def solution(mesh):
    n = mesh.shape["ctx"]

    def per_device(query_rows, key_rows, value_rows, out_grad):
        tok, width = query_rows.shape
        heads = width // DH
        states = pltpu.VMEM((2, heads, DH, DH), F32)
        sems = pltpu.SemaphoreType.DMA((2, heads))
        return pl.pallas_call(
            functools.partial(kernel, n, heads),
            out_shape=[jax.ShapeDtypeStruct((tok, width), F32)] * 3,
            in_specs=[pl.BlockSpec(memory_space=pl.ANY)] * 4,
            out_specs=[pl.BlockSpec(memory_space=pl.ANY)] * 3,
            scratch_shapes=[
                pltpu.VMEM((4, tok, width), BF16),
                states, states, states, states,
                pltpu.VMEM((3, tok, width), F32),
                pltpu.SemaphoreType.DMA((4,)),
                pltpu.SemaphoreType.DMA((3, heads)),
                sems, sems, sems, sems,
            ],
            compiler_params=pltpu.CompilerParams(
                collective_id=0, has_side_effects=True, vmem_limit_bytes=32 << 20
            ),
        )(query_rows, key_rows, value_rows, out_grad)

    spec = P("ctx", "head")
    return jax.shard_map(
        per_device, mesh=mesh, in_specs=(spec,) * 4, out_specs=(spec,) * 3, check_vma=False
    )
```

```python
import functools

import jax
import jax.numpy as jnp
from jax import lax
from jax.experimental import pallas as pl
from jax.experimental.pallas import tpu as pltpu
from jax.sharding import PartitionSpec as P

DH = 128
MESH = pl.DeviceIdType.MESH
F32 = jnp.float32
BF16 = jnp.bfloat16


def dot(left, right, over_left, over_right):
    return lax.dot_general(
        left, right, (((over_left,), (over_right,)), ((), ())), preferred_element_type=F32
    )


def kernel(
    n, heads,
    q_hbm, k_hbm, v_hbm, g_hbm, dq, dk, dv,
    rows, own, partner, carry_in, carry_out,
    load_sem, swap_send, swap_recv, chain_send, chain_recv,
):
    tok = rows.shape[1]
    me = lax.axis_index("ctx")
    side = lax.rem(me, 2)
    row = me // 2
    last = n // 2 - 1
    other = me + 1 - 2 * side

    loads = [
        pltpu.make_async_copy(src, rows.at[i], load_sem.at[i])
        for i, src in enumerate((k_hbm, v_hbm, q_hbm, g_hbm))
    ]
    for load in loads:
        load.start()

    barrier = pltpu.get_barrier_semaphore()

    def greet(device):
        pl.semaphore_signal(barrier, inc=1, device_id={"ctx": device}, device_id_type=MESH)

    greet(other)

    @pl.when(row > 0)
    def _():
        greet(me - 2)

    @pl.when(row < last)
    def _():
        greet(me + 2)

    for load in loads:
        load.wait()

    def swap(kind, h):
        return pltpu.make_async_remote_copy(
            src_ref=own.at[kind, h],
            dst_ref=partner.at[kind, h],
            send_sem=swap_send.at[kind, h],
            recv_sem=swap_recv.at[kind, h],
            device_id={"ctx": other},
            device_id_type=MESH,
        )

    def chain(kind, h):
        return pltpu.make_async_remote_copy(
            src_ref=carry_out.at[kind, h],
            dst_ref=carry_in.at[kind, h],
            send_sem=chain_send.at[kind, h],
            recv_sem=chain_recv.at[kind, h],
            device_id={"ctx": me + 2 - 4 * kind},
            device_id_type=MESH,
        )

    def columns(h):
        return pl.ds(pl.multiple_of(h * DH, DH), DH)

    early = jnp.where(2 * row <= last, 0, 1)

    def edge(kind):
        return jnp.where(kind == 0, last, 0)

    def begin(kind):
        return jnp.where(kind == 0, 0, last)

    def make(kind, h):
        own[kind, h] = dot(rows[2 * kind, :, columns(h)], rows[2 * kind + 1, :, columns(h)], 0, 0)

    def give(kind, h):
        @pl.when((row != edge(kind)) | (side == kind))
        def _():
            swap(kind, h).start()

    def start_swaps(kind, from_head):
        def one(h, _):
            make(kind, h)
            give(kind, h)
            return 0

        lax.fori_loop(from_head, heads, one, 0)

    def carry(kind, h):
        takes = (row != edge(kind)) | (side == 1 - kind)

        @pl.when(takes)
        def _():
            swap(kind, h).wait_recv()

        @pl.when(row != begin(kind))
        def _():
            chain(kind, h).wait_recv()

        before = jnp.where(row != begin(kind), carry_in[kind, h], 0.0)

        @pl.when(row != edge(kind))
        def _():
            carry_out[kind, h] = before + own[kind, h] + partner[kind, h]
            chain(kind, h).start()

        total = before + jnp.where(side == 1 - kind, partner[kind, h], 0.0)
        total = total.astype(BF16)

        @pl.when(kind == 0)
        def _():
            dq[:, columns(h)] += dot(rows[3, :, columns(h)], total, 1, 1)

        @pl.when(kind == 1)
        def _():
            dk[:, columns(h)] += dot(rows[1, :, columns(h)], total, 1, 1)
            dv[:, columns(h)] += dot(rows[0, :, columns(h)], total, 1, 0)

    make(early, 0)
    peers = 1 + jnp.where(row > 0, 1, 0) + jnp.where(row < last, 1, 0)
    pl.semaphore_wait(barrier, peers)
    give(early, 0)
    start_swaps(early, 1)
    start_swaps(1 - early, 0)

    down = lax.broadcasted_iota(jnp.int32, (tok, tok), 0)
    across = lax.broadcasted_iota(jnp.int32, (tok, tok), 1)

    def first(h, _):
        k, v, q, g = (rows[i, :, columns(h)] for i in range(4))
        dprob = jnp.where(down >= across, dot(g, v, 1, 1), 0.0).astype(BF16)
        dprob_t = jnp.where(down <= across, dot(v, g, 1, 1), 0.0).astype(BF16)
        scores_t = jnp.where(down <= across, dot(k, q, 1, 1), 0.0).astype(BF16)
        dq[:, columns(h)] = dot(dprob, k, 1, 0)
        dk[:, columns(h)] = dot(dprob_t, q, 1, 0)
        dv[:, columns(h)] = dot(scores_t, g, 1, 0)
        carry(early, h)
        return 0

    lax.fori_loop(0, heads, first, 0)

    def second(h, _):
        carry(1 - early, h)
        return 0

    lax.fori_loop(0, heads, second, 0)

    def drain(h, _):
        for kind in range(2):
            @pl.when((row != edge(kind)) | (side == kind))
            def _():
                swap(kind, h).wait_send()

            @pl.when(row != edge(kind))
            def _():
                chain(kind, h).wait_send()

        return 0

    lax.fori_loop(0, heads, drain, 0)


def deliver(dq, dk, dv, dq_hbm, dk_hbm, dv_hbm, sems):
    copies = [
        pltpu.make_async_copy(src, dst, sems.at[i])
        for i, (src, dst) in enumerate(((dq, dq_hbm), (dk, dk_hbm), (dv, dv_hbm)))
    ]
    for copy in copies:
        copy.start()
    for copy in copies:
        copy.wait()


def solution(mesh):
    n = mesh.shape["ctx"]

    def per_device(query_rows, key_rows, value_rows, out_grad):
        tok, width = query_rows.shape
        heads = width // DH
        states = pltpu.VMEM((2, heads, DH, DH), F32)
        sems = pltpu.SemaphoreType.DMA((2, heads))
        results = pl.pallas_call(
            functools.partial(kernel, n, heads),
            out_shape=[pltpu.VMEM((tok, width), F32)] * 3,
            in_specs=[pl.BlockSpec(memory_space=pltpu.HBM)] * 4,
            out_specs=[pl.BlockSpec(memory_space=pltpu.VMEM)] * 3,
            scratch_shapes=[
                pltpu.VMEM((4, tok, width), BF16),
                states, states, states, states,
                pltpu.SemaphoreType.DMA((4,)),
                sems, sems, sems, sems,
            ],
            compiler_params=pltpu.CompilerParams(
                collective_id=0, has_side_effects=True, vmem_limit_bytes=60 << 20
            ),
        )(query_rows, key_rows, value_rows, out_grad)
        return pl.pallas_call(
            deliver,
            out_shape=[jax.ShapeDtypeStruct((tok, width), F32)] * 3,
            in_specs=[pl.BlockSpec(memory_space=pl.ANY)] * 3,
            out_specs=[pl.BlockSpec(memory_space=pltpu.HBM)] * 3,
            scratch_shapes=[pltpu.SemaphoreType.DMA((3,))],
            compiler_params=pltpu.CompilerParams(vmem_limit_bytes=1 << 20),
        )(*results)

    spec = P("ctx", "head")
    return jax.shard_map(
        per_device, mesh=mesh, in_specs=(spec,) * 4, out_specs=(spec,) * 3, check_vma=False
    )
```

```python
import functools

import jax
import jax.numpy as jnp
from jax import lax
from jax.experimental import pallas as pl
from jax.experimental.pallas import tpu as pltpu
from jax.sharding import PartitionSpec as P

DH = 128
MESH = pl.DeviceIdType.MESH
F32 = jnp.float32
BF16 = jnp.bfloat16


def dot(left, right, over_left, over_right):
    return lax.dot_general(
        left, right, (((over_left,), (over_right,)), ((), ())), preferred_element_type=F32
    )


def kernel(
    n, heads,
    q_hbm, k_hbm, v_hbm, g_hbm, dq, dk, dv,
    rows, own, partner, carry_in, carry_out,
    load_sem, swap_send, swap_recv, chain_send, chain_recv,
):
    tok = rows.shape[1]
    me = lax.axis_index("ctx")
    side = lax.rem(me, 2)
    row = me // 2
    last = n // 2 - 1
    other = me + 1 - 2 * side

    loads = [
        pltpu.make_async_copy(src, rows.at[i], load_sem.at[i])
        for i, src in enumerate((k_hbm, v_hbm, q_hbm, g_hbm))
    ]
    for load in loads:
        load.start()

    barrier = pltpu.get_barrier_semaphore()

    def greet(device):
        pl.semaphore_signal(barrier, inc=1, device_id={"ctx": device}, device_id_type=MESH)

    greet(other)

    @pl.when(row > 0)
    def _():
        greet(me - 2)

    @pl.when(row < last)
    def _():
        greet(me + 2)

    for load in loads:
        load.wait()

    def swap(source, kind, h):
        return pltpu.make_async_remote_copy(
            src_ref=source.at[kind, h],
            dst_ref=partner.at[kind, h],
            send_sem=swap_send.at[kind, h],
            recv_sem=swap_recv.at[kind, h],
            device_id={"ctx": other},
            device_id_type=MESH,
        )

    def chain(kind, h):
        return pltpu.make_async_remote_copy(
            src_ref=carry_out.at[kind, h],
            dst_ref=carry_in.at[kind, h],
            send_sem=chain_send.at[kind, h],
            recv_sem=chain_recv.at[kind, h],
            device_id={"ctx": me + 2 - 4 * kind},
            device_id_type=MESH,
        )

    def columns(h):
        return pl.ds(pl.multiple_of(h * DH, DH), DH)

    early = jnp.where(2 * row <= last, 0, 1)

    def place(kind):
        return jnp.where(kind == 0, row, last - row)

    def lean(kind):
        return side == 1 - kind

    third = 3 * heads // 8

    def skip(h):
        late = jnp.where(h < third, 2, jnp.where(h < 2 * third, 1, 0))
        return jnp.maximum(last - late, 0)

    def make(kind, h):
        own[kind, h] = dot(rows[2 * kind, :, columns(h)], rows[2 * kind + 1, :, columns(h)], 0, 0)

    def give(kind, h):
        @pl.when((side == kind) | (place(kind) < skip(h)))
        def _():
            swap(own, kind, h).start()

    def start_swaps(kind, from_head):
        def one(h, _):
            make(kind, h)
            give(kind, h)
            return 0

        lax.fori_loop(from_head, heads, one, 0)

    def carry(kind, h):
        at, stop, thin = place(kind), skip(h), lean(kind)
        inside = thin | (at <= stop)

        @pl.when((at > 0) & inside)
        def _():
            chain(kind, h).wait_recv()

        @pl.when((at > stop) & thin)
        def _():
            swap(carry_in, kind, h).start()

        @pl.when((at != stop) | thin)
        def _():
            swap(own, kind, h).wait_recv()

        before = jnp.where(inside, jnp.where(at > 0, carry_in[kind, h], 0.0), partner[kind, h])

        @pl.when(jnp.where(thin, at < last, at < stop))
        def _():
            carry_out[kind, h] = before + own[kind, h] + partner[kind, h]
            chain(kind, h).start()

        total = before + jnp.where(thin, partner[kind, h], 0.0)
        total = total.astype(BF16)

        @pl.when(kind == 0)
        def _():
            dq[:, columns(h)] += dot(rows[3, :, columns(h)], total, 1, 1)

        @pl.when(kind == 1)
        def _():
            dk[:, columns(h)] += dot(rows[1, :, columns(h)], total, 1, 1)
            dv[:, columns(h)] += dot(rows[0, :, columns(h)], total, 1, 0)

    make(early, 0)
    peers = 1 + jnp.where(row > 0, 1, 0) + jnp.where(row < last, 1, 0)
    pl.semaphore_wait(barrier, peers)
    give(early, 0)
    start_swaps(early, 1)
    start_swaps(1 - early, 0)

    down = lax.broadcasted_iota(jnp.int32, (tok, tok), 0)
    across = lax.broadcasted_iota(jnp.int32, (tok, tok), 1)

    def first(h, _):
        k, v, q, g = (rows[i, :, columns(h)] for i in range(4))
        dprob = jnp.where(down >= across, dot(g, v, 1, 1), 0.0).astype(BF16)
        dprob_t = jnp.where(down <= across, dot(v, g, 1, 1), 0.0).astype(BF16)
        scores_t = jnp.where(down <= across, dot(k, q, 1, 1), 0.0).astype(BF16)
        dq[:, columns(h)] = dot(dprob, k, 1, 0)
        dk[:, columns(h)] = dot(dprob_t, q, 1, 0)
        dv[:, columns(h)] = dot(scores_t, g, 1, 0)
        carry(early, h)
        return 0

    lax.fori_loop(0, heads, first, 0)

    def second(h, _):
        carry(1 - early, h)
        return 0

    lax.fori_loop(0, heads, second, 0)

    def drain(h, _):
        for kind in range(2):
            at, stop, thin = place(kind), skip(h), lean(kind)

            @pl.when((at != stop) | ~thin)
            def _():
                swap(own, kind, h).wait_send()

            @pl.when(jnp.where(thin, at < last, at < stop))
            def _():
                chain(kind, h).wait_send()

        return 0

    lax.fori_loop(0, heads, drain, 0)


def deliver(dq, dk, dv, dq_hbm, dk_hbm, dv_hbm, sems):
    copies = [
        pltpu.make_async_copy(src, dst, sems.at[i])
        for i, (src, dst) in enumerate(((dq, dq_hbm), (dk, dk_hbm), (dv, dv_hbm)))
    ]
    for copy in copies:
        copy.start()
    for copy in copies:
        copy.wait()


def solution(mesh):
    n = mesh.shape["ctx"]

    def per_device(query_rows, key_rows, value_rows, out_grad):
        tok, width = query_rows.shape
        heads = width // DH
        states = pltpu.VMEM((2, heads, DH, DH), F32)
        sems = pltpu.SemaphoreType.DMA((2, heads))
        results = pl.pallas_call(
            functools.partial(kernel, n, heads),
            out_shape=[pltpu.VMEM((tok, width), F32)] * 3,
            in_specs=[pl.BlockSpec(memory_space=pltpu.HBM)] * 4,
            out_specs=[pl.BlockSpec(memory_space=pltpu.VMEM)] * 3,
            scratch_shapes=[
                pltpu.VMEM((4, tok, width), BF16),
                states, states, states, states,
                pltpu.SemaphoreType.DMA((4,)),
                sems, sems, sems, sems,
            ],
            compiler_params=pltpu.CompilerParams(
                collective_id=0, has_side_effects=True, vmem_limit_bytes=60 << 20
            ),
        )(query_rows, key_rows, value_rows, out_grad)
        return pl.pallas_call(
            deliver,
            out_shape=[jax.ShapeDtypeStruct((tok, width), F32)] * 3,
            in_specs=[pl.BlockSpec(memory_space=pl.ANY)] * 3,
            out_specs=[pl.BlockSpec(memory_space=pltpu.HBM)] * 3,
            scratch_shapes=[pltpu.SemaphoreType.DMA((3,))],
            compiler_params=pltpu.CompilerParams(vmem_limit_bytes=1 << 20),
        )(*results)

    spec = P("ctx", "head")
    return jax.shard_map(
        per_device, mesh=mesh, in_specs=(spec,) * 4, out_specs=(spec,) * 3, check_vma=False
    )
```

```python
import functools

import jax
import jax.numpy as jnp
from jax import lax
from jax.experimental import pallas as pl
from jax.experimental.pallas import tpu as pltpu
from jax.sharding import PartitionSpec as P

DH = 128
LAG = 4
MESH = pl.DeviceIdType.MESH
F32 = jnp.float32
BF16 = jnp.bfloat16


def dot(left, right, over_left, over_right):
    return lax.dot_general(
        left, right, (((over_left,), (over_right,)), ((), ())), preferred_element_type=F32
    )


def kernel(
    n, heads,
    q_hbm, k_hbm, v_hbm, g_hbm, dq, dk, dv,
    rows, own, partner, carry_in, carry_out,
    load_sem, swap_send, swap_recv, chain_send, chain_recv,
):
    tok = rows.shape[1]
    me = lax.axis_index("ctx")
    side = lax.rem(me, 2)
    row = me // 2
    last = n // 2 - 1
    other = me + 1 - 2 * side

    loads = [
        pltpu.make_async_copy(src, rows.at[i], load_sem.at[i])
        for i, src in enumerate((k_hbm, v_hbm, q_hbm, g_hbm))
    ]
    for load in loads:
        load.start()

    barrier = pltpu.get_barrier_semaphore()

    def greet(device):
        pl.semaphore_signal(barrier, inc=1, device_id={"ctx": device}, device_id_type=MESH)

    greet(other)

    @pl.when(row > 0)
    def _():
        greet(me - 2)

    @pl.when(row < last)
    def _():
        greet(me + 2)

    for load in loads:
        load.wait()

    def swap(source, kind, h):
        return pltpu.make_async_remote_copy(
            src_ref=source.at[kind, h],
            dst_ref=partner.at[kind, h],
            send_sem=swap_send.at[kind, h],
            recv_sem=swap_recv.at[kind, h],
            device_id={"ctx": other},
            device_id_type=MESH,
        )

    def chain(kind, h):
        return pltpu.make_async_remote_copy(
            src_ref=carry_out.at[kind, h],
            dst_ref=carry_in.at[kind, h],
            send_sem=chain_send.at[kind, h],
            recv_sem=chain_recv.at[kind, h],
            device_id={"ctx": me + 2 - 4 * kind},
            device_id_type=MESH,
        )

    def columns(h):
        return pl.ds(pl.multiple_of(h * DH, DH), DH)

    early = jnp.where(2 * row <= last, 0, 1)

    def place(kind):
        return jnp.where(kind == 0, row, last - row)

    def lean(kind):
        return side == 1 - kind

    third = 3 * heads // 8

    def skip(h):
        short = jnp.where(h < third, 2, jnp.where(h < 2 * third, 1, 0))
        return jnp.maximum(last - short, 0)

    def make(kind, h):
        own[kind, h] = dot(rows[2 * kind, :, columns(h)], rows[2 * kind + 1, :, columns(h)], 0, 0)

    def give(kind, h):
        @pl.when((side == kind) | (place(kind) < skip(h)))
        def _():
            swap(own, kind, h).start()

    def start_swaps(kind, from_head):
        def one(h, _):
            make(kind, h)
            give(kind, h)
            return 0

        lax.fori_loop(from_head, heads, one, 0)

    def carry(kind, h):
        at, stop, thin = place(kind), skip(h), lean(kind)
        inside = thin | (at <= stop)

        @pl.when((at > 0) & inside)
        def _():
            chain(kind, h).wait_recv()

        @pl.when((at > stop) & thin)
        def _():
            swap(carry_in, kind, h).start()

        @pl.when((at != stop) | thin)
        def _():
            swap(own, kind, h).wait_recv()

        before = jnp.where(inside, jnp.where(at > 0, carry_in[kind, h], 0.0), partner[kind, h])

        @pl.when(jnp.where(thin, at < last, at < stop))
        def _():
            carry_out[kind, h] = before + own[kind, h] + partner[kind, h]
            chain(kind, h).start()

        total = before + jnp.where(thin, partner[kind, h], 0.0)
        total = total.astype(BF16)

        @pl.when(kind == 0)
        def _():
            dq[:, columns(h)] += dot(rows[3, :, columns(h)], total, 1, 1)

        @pl.when(kind == 1)
        def _():
            dk[:, columns(h)] += dot(rows[1, :, columns(h)], total, 1, 1)
            dv[:, columns(h)] += dot(rows[0, :, columns(h)], total, 1, 0)

    make(early, 0)
    peers = 1 + jnp.where(row > 0, 1, 0) + jnp.where(row < last, 1, 0)
    pl.semaphore_wait(barrier, peers)
    give(early, 0)
    start_swaps(early, 1)
    start_swaps(1 - early, 0)

    down = lax.broadcasted_iota(jnp.int32, (tok, tok), 0)
    across = lax.broadcasted_iota(jnp.int32, (tok, tok), 1)

    def in_block(h):
        k, v, q, g = (rows[i, :, columns(h)] for i in range(4))
        dprob = jnp.where(down >= across, dot(g, v, 1, 1), 0.0).astype(BF16)
        dprob_t = jnp.where(down <= across, dot(v, g, 1, 1), 0.0).astype(BF16)
        scores_t = jnp.where(down <= across, dot(k, q, 1, 1), 0.0).astype(BF16)
        dq[:, columns(h)] = dot(dprob, k, 1, 0)
        dk[:, columns(h)] = dot(dprob_t, q, 1, 0)
        dv[:, columns(h)] = dot(scores_t, g, 1, 0)

    late = 1 - early
    lag = jnp.where((place(early) == 0) | (side == late), heads, min(LAG, heads))
    turn = jnp.where(side == late, 2 * third, 0)

    def step(t, _):
        @pl.when(t < heads)
        def _():
            in_block(t)
            carry(early, t)

        @pl.when((t >= lag) & (t < lag + heads))
        def _():
            carry(late, lax.rem(t - lag + turn, heads))

        return 0

    lax.fori_loop(0, 2 * heads, step, 0)

    def drain(h, _):
        for kind in range(2):
            at, stop, thin = place(kind), skip(h), lean(kind)

            @pl.when((at != stop) | ~thin)
            def _():
                swap(own, kind, h).wait_send()

            @pl.when(jnp.where(thin, at < last, at < stop))
            def _():
                chain(kind, h).wait_send()

        return 0

    lax.fori_loop(0, heads, drain, 0)


def deliver(dq, dk, dv, dq_hbm, dk_hbm, dv_hbm, sems):
    copies = [
        pltpu.make_async_copy(src, dst, sems.at[i])
        for i, (src, dst) in enumerate(((dq, dq_hbm), (dk, dk_hbm), (dv, dv_hbm)))
    ]
    for copy in copies:
        copy.start()
    for copy in copies:
        copy.wait()


def solution(mesh):
    n = mesh.shape["ctx"]

    def per_device(query_rows, key_rows, value_rows, out_grad):
        tok, width = query_rows.shape
        heads = width // DH
        states = pltpu.VMEM((2, heads, DH, DH), F32)
        sems = pltpu.SemaphoreType.DMA((2, heads))
        results = pl.pallas_call(
            functools.partial(kernel, n, heads),
            out_shape=[pltpu.VMEM((tok, width), F32)] * 3,
            in_specs=[pl.BlockSpec(memory_space=pltpu.HBM)] * 4,
            out_specs=[pl.BlockSpec(memory_space=pltpu.VMEM)] * 3,
            scratch_shapes=[
                pltpu.VMEM((4, tok, width), BF16),
                states, states, states, states,
                pltpu.SemaphoreType.DMA((4,)),
                sems, sems, sems, sems,
            ],
            compiler_params=pltpu.CompilerParams(
                collective_id=0, has_side_effects=True, vmem_limit_bytes=60 << 20
            ),
        )(query_rows, key_rows, value_rows, out_grad)
        return pl.pallas_call(
            deliver,
            out_shape=[jax.ShapeDtypeStruct((tok, width), F32)] * 3,
            in_specs=[pl.BlockSpec(memory_space=pl.ANY)] * 3,
            out_specs=[pl.BlockSpec(memory_space=pltpu.HBM)] * 3,
            scratch_shapes=[pltpu.SemaphoreType.DMA((3,))],
            compiler_params=pltpu.CompilerParams(vmem_limit_bytes=1 << 20),
        )(*results)

    spec = P("ctx", "head")
    return jax.shard_map(
        per_device, mesh=mesh, in_specs=(spec,) * 4, out_specs=(spec,) * 3, check_vma=False
    )
```

```python
import functools

import jax
import jax.numpy as jnp
from jax import lax
from jax.experimental import pallas as pl
from jax.experimental.pallas import tpu as pltpu
from jax.sharding import PartitionSpec as P

DH = 128
LAG = 3
MESH = pl.DeviceIdType.MESH
F32 = jnp.float32
BF16 = jnp.bfloat16


def dot(left, right, over_left, over_right):
    return lax.dot_general(
        left, right, (((over_left,), (over_right,)), ((), ())), preferred_element_type=F32
    )


def kernel(
    n, heads,
    q_hbm, k_hbm, v_hbm, g_hbm, dq, dk, dv,
    rows, own, partner, carry_in, carry_out,
    load_sem, swap_send, swap_recv, chain_send, chain_recv,
):
    tok = rows.shape[1]
    me = lax.axis_index("ctx")
    side = lax.rem(me, 2)
    row = me // 2
    last = n // 2 - 1
    other = me + 1 - 2 * side

    loads = [
        pltpu.make_async_copy(src, rows.at[i], load_sem.at[i])
        for i, src in enumerate((k_hbm, v_hbm, q_hbm, g_hbm))
    ]
    for load in loads:
        load.start()

    barrier = pltpu.get_barrier_semaphore()

    def greet(device):
        pl.semaphore_signal(barrier, inc=1, device_id={"ctx": device}, device_id_type=MESH)

    greet(other)

    @pl.when(row > 0)
    def _():
        greet(me - 2)

    @pl.when(row < last)
    def _():
        greet(me + 2)

    for load in loads:
        load.wait()

    def swap(source, kind, h):
        return pltpu.make_async_remote_copy(
            src_ref=source.at[kind, h],
            dst_ref=partner.at[kind, h],
            send_sem=swap_send.at[kind, h],
            recv_sem=swap_recv.at[kind, h],
            device_id={"ctx": other},
            device_id_type=MESH,
        )

    def chain(kind, h):
        return pltpu.make_async_remote_copy(
            src_ref=carry_out.at[kind, h],
            dst_ref=carry_in.at[kind, h],
            send_sem=chain_send.at[kind, h],
            recv_sem=chain_recv.at[kind, h],
            device_id={"ctx": me + 2 - 4 * kind},
            device_id_type=MESH,
        )

    def columns(h):
        return pl.ds(pl.multiple_of(h * DH, DH), DH)

    early = jnp.where(2 * row <= last, 0, 1)

    def place(kind):
        return jnp.where(kind == 0, row, last - row)

    def lean(kind):
        return side == 1 - kind

    third = 3 * heads // 8

    def skip(h):
        short = jnp.where(h < third, 2, jnp.where(h < 2 * third, 1, 0))
        return jnp.maximum(last - short, 0)

    def make(kind, h):
        own[kind, h] = dot(rows[2 * kind, :, columns(h)], rows[2 * kind + 1, :, columns(h)], 0, 0)

    def give(kind, h):
        @pl.when((side == kind) | (place(kind) < skip(h)))
        def _():
            swap(own, kind, h).start()

    def start_swaps(kind, from_head):
        def one(h, _):
            make(kind, h)
            give(kind, h)
            return 0

        lax.fori_loop(from_head, heads, one, 0)

    def carry(kind, h):
        at, stop, thin = place(kind), skip(h), lean(kind)
        inside = thin | (at <= stop)

        @pl.when((at > 0) & inside)
        def _():
            chain(kind, h).wait_recv()

        @pl.when((at > stop) & thin)
        def _():
            swap(carry_in, kind, h).start()

        @pl.when((at != stop) | thin)
        def _():
            swap(own, kind, h).wait_recv()

        before = jnp.where(inside, jnp.where(at > 0, carry_in[kind, h], 0.0), partner[kind, h])

        @pl.when(jnp.where(thin, at < last, at < stop))
        def _():
            carry_out[kind, h] = before + own[kind, h] + partner[kind, h]
            chain(kind, h).start()

        total = before + jnp.where(thin, partner[kind, h], 0.0)
        total = total.astype(BF16)

        @pl.when(kind == 0)
        def _():
            dq[:, columns(h)] += dot(rows[3, :, columns(h)], total, 1, 1)

        @pl.when(kind == 1)
        def _():
            dk[:, columns(h)] += dot(rows[1, :, columns(h)], total, 1, 1)
            dv[:, columns(h)] += dot(rows[0, :, columns(h)], total, 1, 0)

    make(early, 0)
    peers = 1 + jnp.where(row > 0, 1, 0) + jnp.where(row < last, 1, 0)
    pl.semaphore_wait(barrier, peers)
    give(early, 0)
    start_swaps(early, 1)
    start_swaps(1 - early, 0)

    down = lax.broadcasted_iota(jnp.int32, (tok, tok), 0)
    across = lax.broadcasted_iota(jnp.int32, (tok, tok), 1)

    def in_block(h):
        k, v, q, g = (rows[i, :, columns(h)] for i in range(4))
        dprob = jnp.where(down >= across, dot(g, v, 1, 1), 0.0).astype(BF16)
        dprob_t = jnp.where(down <= across, dot(v, g, 1, 1), 0.0).astype(BF16)
        scores_t = jnp.where(down <= across, dot(k, q, 1, 1), 0.0).astype(BF16)
        dq[:, columns(h)] = dot(dprob, k, 1, 0)
        dk[:, columns(h)] = dot(dprob_t, q, 1, 0)
        dv[:, columns(h)] = dot(scores_t, g, 1, 0)

    late = 1 - early
    lag = jnp.where((place(early) == 0) | (side == late), heads, min(LAG, heads))
    turn = jnp.where(side == late, 2 * third, 0)

    def step(t, _):
        @pl.when(t < heads)
        def _():
            in_block(t)
            carry(early, t)

        @pl.when((t >= lag) & (t < lag + heads))
        def _():
            carry(late, lax.rem(t - lag + turn, heads))

        return 0

    lax.fori_loop(0, 2 * heads, step, 0)

    def drain(h, _):
        for kind in range(2):
            at, stop, thin = place(kind), skip(h), lean(kind)

            @pl.when((at != stop) | ~thin)
            def _():
                swap(own, kind, h).wait_send()

            @pl.when(jnp.where(thin, at < last, at < stop))
            def _():
                chain(kind, h).wait_send()

        return 0

    lax.fori_loop(0, heads, drain, 0)


def deliver(dq, dk, dv, dq_hbm, dk_hbm, dv_hbm, sems):
    copies = [
        pltpu.make_async_copy(src, dst, sems.at[i])
        for i, (src, dst) in enumerate(((dq, dq_hbm), (dk, dk_hbm), (dv, dv_hbm)))
    ]
    for copy in copies:
        copy.start()
    for copy in copies:
        copy.wait()


def solution(mesh):
    n = mesh.shape["ctx"]

    def per_device(query_rows, key_rows, value_rows, out_grad):
        tok, width = query_rows.shape
        heads = width // DH
        states = pltpu.VMEM((2, heads, DH, DH), F32)
        sems = pltpu.SemaphoreType.DMA((2, heads))
        results = pl.pallas_call(
            functools.partial(kernel, n, heads),
            out_shape=[pltpu.VMEM((tok, width), F32)] * 3,
            in_specs=[pl.BlockSpec(memory_space=pltpu.HBM)] * 4,
            out_specs=[pl.BlockSpec(memory_space=pltpu.VMEM)] * 3,
            scratch_shapes=[
                pltpu.VMEM((4, tok, width), BF16),
                states, states, states, states,
                pltpu.SemaphoreType.DMA((4,)),
                sems, sems, sems, sems,
            ],
            compiler_params=pltpu.CompilerParams(
                collective_id=0, has_side_effects=True, vmem_limit_bytes=60 << 20
            ),
        )(query_rows, key_rows, value_rows, out_grad)
        return pl.pallas_call(
            deliver,
            out_shape=[jax.ShapeDtypeStruct((tok, width), F32)] * 3,
            in_specs=[pl.BlockSpec(memory_space=pl.ANY)] * 3,
            out_specs=[pl.BlockSpec(memory_space=pltpu.HBM)] * 3,
            scratch_shapes=[pltpu.SemaphoreType.DMA((3,))],
            compiler_params=pltpu.CompilerParams(vmem_limit_bytes=1 << 20),
        )(*results)

    spec = P("ctx", "head")
    return jax.shard_map(
        per_device, mesh=mesh, in_specs=(spec,) * 4, out_specs=(spec,) * 3, check_vma=False
    )
```

```python
import functools

import jax
import jax.numpy as jnp
from jax import lax
from jax.experimental import pallas as pl
from jax.experimental.pallas import tpu as pltpu
from jax.sharding import PartitionSpec as P

DH = 128
LAG = 3
MESH = pl.DeviceIdType.MESH
F32 = jnp.float32
BF16 = jnp.bfloat16


def dot(left, right, over_left, over_right):
    return lax.dot_general(
        left, right, (((over_left,), (over_right,)), ((), ())), preferred_element_type=F32
    )


def kernel(
    n, heads,
    q_hbm, k_hbm, v_hbm, g_hbm, dq, dk, dv,
    rows, own, partner, carry_in, carry_out,
    load_sem, swap_send, swap_recv, chain_send, chain_recv,
):
    tok = rows.shape[1]
    me = lax.axis_index("ctx")
    side = lax.rem(me, 2)
    row = me // 2
    last = n // 2 - 1
    other = me + 1 - 2 * side

    loads = [
        pltpu.make_async_copy(src, rows.at[i], load_sem.at[i])
        for i, src in enumerate((k_hbm, v_hbm, q_hbm, g_hbm))
    ]
    early = jnp.where(2 * row <= last, 0, 1)

    def of_kind(kind, act):
        for k in range(2):
            @pl.when(kind == k)
            def _():
                act(loads[2 * k])
                act(loads[2 * k + 1])

    of_kind(early, lambda load: load.start())
    of_kind(1 - early, lambda load: load.start())

    barrier = pltpu.get_barrier_semaphore()

    def greet(device):
        pl.semaphore_signal(barrier, inc=1, device_id={"ctx": device}, device_id_type=MESH)

    greet(other)

    @pl.when(row > 0)
    def _():
        greet(me - 2)

    @pl.when(row < last)
    def _():
        greet(me + 2)

    of_kind(early, lambda load: load.wait())

    def swap(source, kind, h):
        return pltpu.make_async_remote_copy(
            src_ref=source.at[kind, h],
            dst_ref=partner.at[kind, h],
            send_sem=swap_send.at[kind, h],
            recv_sem=swap_recv.at[kind, h],
            device_id={"ctx": other},
            device_id_type=MESH,
        )

    def chain(kind, h):
        return pltpu.make_async_remote_copy(
            src_ref=carry_out.at[kind, h],
            dst_ref=carry_in.at[kind, h],
            send_sem=chain_send.at[kind, h],
            recv_sem=chain_recv.at[kind, h],
            device_id={"ctx": me + 2 - 4 * kind},
            device_id_type=MESH,
        )

    def columns(h):
        return pl.ds(pl.multiple_of(h * DH, DH), DH)


    def place(kind):
        return jnp.where(kind == 0, row, last - row)

    def lean(kind):
        return side == 1 - kind

    third = 3 * heads // 8

    def skip(h):
        short = jnp.where(h < third, 2, jnp.where(h < 2 * third, 1, 0))
        return jnp.maximum(last - short, 0)

    def make(kind, h):
        own[kind, h] = dot(rows[2 * kind, :, columns(h)], rows[2 * kind + 1, :, columns(h)], 0, 0)

    def give(kind, h):
        @pl.when((side == kind) | (place(kind) < skip(h)))
        def _():
            swap(own, kind, h).start()

    def start_swaps(kind, from_head):
        def one(h, _):
            make(kind, h)
            give(kind, h)
            return 0

        lax.fori_loop(from_head, heads, one, 0)

    def carry(kind, h):
        at, stop, thin = place(kind), skip(h), lean(kind)
        inside = thin | (at <= stop)

        @pl.when((at > 0) & inside)
        def _():
            chain(kind, h).wait_recv()

        @pl.when((at > stop) & thin)
        def _():
            swap(carry_in, kind, h).start()

        @pl.when((at != stop) | thin)
        def _():
            swap(own, kind, h).wait_recv()

        before = jnp.where(inside, jnp.where(at > 0, carry_in[kind, h], 0.0), partner[kind, h])

        @pl.when(jnp.where(thin, at < last, at < stop))
        def _():
            carry_out[kind, h] = before + own[kind, h] + partner[kind, h]
            chain(kind, h).start()

        total = before + jnp.where(thin, partner[kind, h], 0.0)
        total = total.astype(BF16)

        @pl.when(kind == 0)
        def _():
            dq[:, columns(h)] += dot(rows[3, :, columns(h)], total, 1, 1)

        @pl.when(kind == 1)
        def _():
            dk[:, columns(h)] += dot(rows[1, :, columns(h)], total, 1, 1)
            dv[:, columns(h)] += dot(rows[0, :, columns(h)], total, 1, 0)

    make(early, 0)
    peers = 1 + jnp.where(row > 0, 1, 0) + jnp.where(row < last, 1, 0)
    pl.semaphore_wait(barrier, peers)
    give(early, 0)
    start_swaps(early, 1)
    of_kind(1 - early, lambda load: load.wait())
    start_swaps(1 - early, 0)

    down = lax.broadcasted_iota(jnp.int32, (tok, tok), 0)
    across = lax.broadcasted_iota(jnp.int32, (tok, tok), 1)

    def in_block(h):
        k, v, q, g = (rows[i, :, columns(h)] for i in range(4))
        dprob = jnp.where(down >= across, dot(g, v, 1, 1), 0.0).astype(BF16)
        dprob_t = jnp.where(down <= across, dot(v, g, 1, 1), 0.0).astype(BF16)
        scores_t = jnp.where(down <= across, dot(k, q, 1, 1), 0.0).astype(BF16)
        dq[:, columns(h)] = dot(dprob, k, 1, 0)
        dk[:, columns(h)] = dot(dprob_t, q, 1, 0)
        dv[:, columns(h)] = dot(scores_t, g, 1, 0)

    late = 1 - early
    lag = jnp.where((place(early) == 0) | (side == late), heads, min(LAG, heads))
    turn = jnp.where(side == late, 2 * third, 0)

    def step(t, _):
        @pl.when(t < heads)
        def _():
            in_block(t)
            carry(early, t)

        @pl.when((t >= lag) & (t < lag + heads))
        def _():
            carry(late, lax.rem(t - lag + turn, heads))

        return 0

    lax.fori_loop(0, 2 * heads, step, 0)

    def drain(h, _):
        for kind in range(2):
            at, stop, thin = place(kind), skip(h), lean(kind)

            @pl.when((at != stop) | ~thin)
            def _():
                swap(own, kind, h).wait_send()

            @pl.when(jnp.where(thin, at < last, at < stop))
            def _():
                chain(kind, h).wait_send()

        return 0

    lax.fori_loop(0, heads, drain, 0)


def deliver(dq, dk, dv, dq_hbm, dk_hbm, dv_hbm, sems):
    copies = [
        pltpu.make_async_copy(src, dst, sems.at[i])
        for i, (src, dst) in enumerate(((dq, dq_hbm), (dk, dk_hbm), (dv, dv_hbm)))
    ]
    for copy in copies:
        copy.start()
    for copy in copies:
        copy.wait()


def solution(mesh):
    n = mesh.shape["ctx"]

    def per_device(query_rows, key_rows, value_rows, out_grad):
        tok, width = query_rows.shape
        heads = width // DH
        states = pltpu.VMEM((2, heads, DH, DH), F32)
        sems = pltpu.SemaphoreType.DMA((2, heads))
        results = pl.pallas_call(
            functools.partial(kernel, n, heads),
            out_shape=[pltpu.VMEM((tok, width), F32)] * 3,
            in_specs=[pl.BlockSpec(memory_space=pltpu.HBM)] * 4,
            out_specs=[pl.BlockSpec(memory_space=pltpu.VMEM)] * 3,
            scratch_shapes=[
                pltpu.VMEM((4, tok, width), BF16),
                states, states, states, states,
                pltpu.SemaphoreType.DMA((4,)),
                sems, sems, sems, sems,
            ],
            compiler_params=pltpu.CompilerParams(
                collective_id=0, has_side_effects=True, vmem_limit_bytes=60 << 20
            ),
        )(query_rows, key_rows, value_rows, out_grad)
        return pl.pallas_call(
            deliver,
            out_shape=[jax.ShapeDtypeStruct((tok, width), F32)] * 3,
            in_specs=[pl.BlockSpec(memory_space=pl.ANY)] * 3,
            out_specs=[pl.BlockSpec(memory_space=pltpu.HBM)] * 3,
            scratch_shapes=[pltpu.SemaphoreType.DMA((3,))],
            compiler_params=pltpu.CompilerParams(vmem_limit_bytes=1 << 20),
        )(*results)

    spec = P("ctx", "head")
    return jax.shard_map(
        per_device, mesh=mesh, in_specs=(spec,) * 4, out_specs=(spec,) * 3, check_vma=False
    )
```
